32 devices in a mesh: parts: 2 (over x), lat: 8 (over z, y), lev: 2 (over core).
Axes of the slice: x: 2, y: 2, z: 4, core: 2. Of those that a mesh axis runs over, the one named last changes fastest.
Arguments:
- fields: float32 [5, 60, 128, 512], P(None, 'lev', ('parts', 'lat')), parts along dimension 2, may hold values from -6 to 6
- region: int32 [128, 512], P(('parts', 'lat')), parts along dimension 0, may hold values from 0 to 7
- land: int32 [128, 512], P(('parts', 'lat')), parts along dimension 0, may hold values 0 or 1
- coef_table: float32 [60, 8], replicated, may hold values from 0.02 to 0.24
- w_in: bfloat16 [1024, 300], replicated, may hold values from -0.375 to 0.375
- b_in: float32 [1024], replicated, may hold values from -3 to 3
- w_mid: bfloat16 [2, 1024, 1024], replicated, may hold values from -0.1875 to 0.1875
- b_mid: float32 [2, 1024], replicated, may hold values from -3 to 3
- w_out: bfloat16 [300, 1024], replicated, may hold values from -0.1875 to 0.1875
- b_out: float32 [300], replicated, may hold values from -3 to 3
Outputs:
- closure: float32 [5, 60, 128, 512], P(None, 'lev', ('parts', 'lat')), parts along dimension 2
The draws below stay inside these ranges and needn't reach their ends.
There are 2 independent parts, one for each index of `parts`. The reference program is written for one: setup_inputs(seed, part) draws one part's arguments, and reference() takes and returns one part's arrays. A program takes and returns all parts, laid end to end along the dimension named above; an argument that names none is the same for every part. Nothing has to cross between parts.
All inputs are finite; a program needn't handle non-finite values. No bound on the sum of `land` on one device may be relied on, other than what follows from the above.
Results may differ from the reference program's by a relative error of at most 0.0025.
Values may be sent and summed in bfloat16 or wider, within the bound.
A program may use at most 64 MiB of HBM per device.

```python
import math
import jax
import jax.numpy as jnp
from jax import lax

V = 5
L = 60
FEAT = 300
HID = 1024
MIDS = 2
REGIONS = 8
PRE = 4
POST = 2
ROWS = 8
NLON = 512
NLAT = 64
N_LAT = 8


def with_ends(values, rng, least, largest):
    place = [jax.random.randint(jax.random.fold_in(rng, axis), (), 0, length) for axis, length in enumerate(values.shape)]
    main_axis = values.shape.index(max(values.shape))
    next_to = place[:main_axis] + [(place[main_axis] + 1) % values.shape[main_axis]] + place[main_axis + 1:]
    return values.at[tuple(place)].set(least).at[tuple(next_to)].set(largest)


def steps_of(own_key, extent, pieces, low, high):
    factor_of = 1.0
    for position, parts in pieces:
        heights = jax.random.uniform(jax.random.fold_in(jax.random.fold_in(own_key, 6), position), (parts,), jnp.float32, low / len(pieces), high / len(pieces))
        factor_of = factor_of * jnp.repeat(jnp.exp(heights), extent[position] // parts).reshape((-1,) + (1,) * (len(extent) - 1 - position))
    return factor_of


def normal_values(stream_key, shape, spread, reach, split=(), held_as=jnp.bfloat16):
    array = jax.random.normal(stream_key, shape, jnp.float32) * spread
    if len(split) > 0:
        array = steps_of(stream_key, shape, split, -0.22, 0.18) * array
    return jnp.clip(array, min=-reach, max=reach).astype(held_as)


def setup_inputs(seed: int = 0, part: int = 0) -> dict:
    key_of = jax.random.split(jax.random.key(seed), 11)
    own_keys = jax.random.split(jax.random.fold_in(key_of[10], part), 11)
    return {
        "fields": normal_values(own_keys[0], (V, L, NLAT, NLON), 1.0, 6.0, ((1, 2), (2, 8)), jnp.float32),
        "region": with_ends(jax.random.randint(own_keys[1], (NLAT, NLON), 0, REGIONS), jax.random.fold_in(own_keys[1], 1), 0, REGIONS - 1).astype(jnp.int32),
        "land": with_ends((jax.random.randint(own_keys[2], (NLAT, NLON), 0, 10) < 3).astype(jnp.int32), jax.random.fold_in(own_keys[2], 1), 0, 1),
        "coef_table": jnp.clip(jnp.exp(jax.random.uniform(key_of[3], (L, REGIONS), jnp.float32, math.log(0.02), math.log(0.24))), 0.02, 0.24),
        "w_in": normal_values(key_of[4], (HID, FEAT), FEAT ** -0.5, 0.375),
        "b_in": normal_values(key_of[5], (HID,), 0.5, 3.0, (), jnp.float32),
        "w_mid": normal_values(key_of[6], (MIDS, HID, HID), HID ** -0.5, 0.1875),
        "b_mid": normal_values(key_of[7], (MIDS, HID), 0.5, 3.0, (), jnp.float32),
        "w_out": normal_values(key_of[8], (FEAT, HID), HID ** -0.5, 0.1875),
        "b_out": normal_values(key_of[9], (FEAT,), 0.5, 3.0, (), jnp.float32),
    }


def diffuse(fields, coeffs):
    east_face = jnp.sqrt(coeffs * jnp.roll(coeffs, -1, axis=2))
    east_flux = east_face * (jnp.roll(fields, -1, axis=3) - fields)
    zonal = east_flux - jnp.roll(east_flux, 1, axis=3)
    north_face = jnp.sqrt(coeffs[:, :-1] * coeffs[:, 1:])
    north_flux = north_face * (fields[:, :, 1:] - fields[:, :, :-1])
    meridional = north_flux[:, :, 1:] - north_flux[:, :, :-1]
    return fields[:, :, 1:-1] + zonal[:, :, 1:-1] + meridional

def smooth(fields, coeffs, count):
    padded_coeffs = jnp.pad(coeffs, ((0, 0), (1, 1), (0, 0)))
    for sweep_index in range(count):
        fields = diffuse(jnp.pad(fields, ((0, 0), (0, 0), (1, 1), (0, 0))), padded_coeffs)
    return fields

def network(profiles, w_in, b_in, w_mid, b_mid, w_out, b_out):
    shape = profiles.shape
    flat = profiles.reshape(shape[0] * shape[1], shape[2] * shape[3])
    hidden = jax.nn.gelu(jnp.dot(w_in, flat, preferred_element_type=jnp.float32) + b_in[:, None]).astype(jnp.bfloat16)
    for layer_index in range(w_mid.shape[0]):
        hidden = jax.nn.gelu(jnp.dot(w_mid[layer_index], hidden, preferred_element_type=jnp.float32) + b_mid[layer_index][:, None]).astype(jnp.bfloat16)
    output = (jnp.dot(w_out, hidden, preferred_element_type=jnp.float32) + b_out[:, None]).astype(jnp.bfloat16)
    return output.reshape(shape)

def reference(fields, region, land, coef_table, w_in, b_in, w_mid, b_mid, w_out, b_out):
    coeffs = coef_table[:, region] * (1.0 - 0.6 * land.astype(jnp.float32))[None]
    smoothed = smooth(fields, coeffs, PRE)
    profiles = smoothed.astype(jnp.bfloat16)
    blocks = profiles.reshape(V, L, N_LAT, ROWS, NLON).transpose(2, 0, 1, 3, 4)
    results = lax.map(lambda block: network(block, w_in, b_in, w_mid, b_mid, w_out, b_out), blocks)
    fluxes = results.transpose(1, 2, 0, 3, 4).reshape(V, L, N_LAT * ROWS, NLON)
    return smooth(fluxes.astype(jnp.float32), coeffs, POST)
```

```python
import functools

import jax
import jax.numpy as jnp
from jax import lax
from jax.experimental import pallas as pl
from jax.experimental.pallas import tpu as pltpu
from jax.sharding import PartitionSpec as P

PRE = 4
POST = 2
MESH = pl.DeviceIdType.MESH
BF = jnp.bfloat16
F32 = jnp.float32


def gelu(x):
    scale = 0.7978845608028654
    inner = x * (scale + (scale * 0.044715) * (x * x))
    half = 0.5 * x
    return half + half * jnp.tanh(inner)


def kernel(
    n_lat, n_var, n_lev, n_row,
    region, land, table, bias, fields, w_in_hbm, w_mid_hbm, w_out_hbm,
    out,
    split, w_in, w_mid, w_out, wi, wo,
    sent, halo, marks, f0, f1, f2, f3, ef, nf, prof, other, h1, h2, flux_own, flux,
    in_sem, out_sem, w_sem, mark_send, mark_recv, halo_send, halo_recv, prof_send, prof_recv,
    flux_send, flux_recv, edge_send, edge_recv,
):
    lat = lax.axis_index("lat")
    lev = lax.axis_index("lev")
    peer = 1 - lev
    has_up = lat > 0
    has_down = lat < n_lat - 1
    pad_lev = table.shape[1]
    feat = n_var * pad_lev
    n_lon = out.shape[1]
    hid = w_mid.shape[1]
    n_mid = w_mid.shape[0]
    half = n_row // 2
    first = PRE
    last = PRE + n_row - 1

    lanes = split.shape[2]
    n_split = split.shape[0]

    def columns_of(ref, c):
        return ref.at[:, c * lanes : (c + 1) * lanes]

    pieces = [
        pltpu.make_async_copy(columns_of(fields, c), split.at[c], in_sem.at[c])
        for c in range(n_split)
    ]
    for piece in pieces:
        piece.start()
    loads = [
        pltpu.make_async_copy(w_in_hbm, w_in, w_sem.at[0]),
        pltpu.make_async_copy(w_out_hbm, w_out, w_sem.at[1]),
        pltpu.make_async_copy(w_mid_hbm, w_mid, w_sem.at[2]),
    ]
    for load in loads:
        load.start()

    barrier = pltpu.get_barrier_semaphore()
    pl.semaphore_signal(barrier, inc=1, device_id={"lev": peer}, device_id_type=MESH)

    @pl.when(has_up)
    def _():
        for j in range(2):
            pl.semaphore_signal(
                barrier, inc=1, device_id={"lat": lat - 1, "lev": j}, device_id_type=MESH
            )

    @pl.when(has_down)
    def _():
        for j in range(2):
            pl.semaphore_signal(
                barrier, inc=1, device_id={"lat": lat + 1, "lev": j}, device_id_type=MESH
            )

    def take_row(r):
        for v in range(n_var):
            base = v * n_lev * n_row
            values = jnp.concatenate(
                [split[c, pl.ds(base + r, n_lev, stride=n_row), :] for c in range(n_split)],
                axis=1,
            )
            values = jnp.concatenate(
                [values, jnp.zeros((pad_lev - n_lev, n_lon), F32)], axis=0
            )
            f0[PRE + r, v * pad_lev : (v + 1) * pad_lev, :] = values
            sent[r, v * pad_lev : (v + 1) * pad_lev, :] = values.astype(BF)

    def row_up(k):
        return pltpu.make_async_remote_copy(
            src_ref=sent.at[k], dst_ref=halo.at[1, k],
            send_sem=halo_send.at[1, k], recv_sem=halo_recv.at[1, k],
            device_id={"lat": lat - 1}, device_id_type=MESH,
        )

    def row_down(k):
        return pltpu.make_async_remote_copy(
            src_ref=sent.at[n_row - 1 - k], dst_ref=halo.at[0, k],
            send_sem=halo_send.at[0, k], recv_sem=halo_recv.at[0, k],
            device_id={"lat": lat + 1}, device_id_type=MESH,
        )

    def marks_to(side, which, source, target):
        return pltpu.make_async_remote_copy(
            src_ref=source, dst_ref=marks.at[side, which],
            send_sem=mark_send.at[side, which], recv_sem=mark_recv.at[side, which],
            device_id={"lat": target}, device_id_type=MESH,
        )

    for piece in pieces:
        piece.wait()
    take_row(0)
    take_row(n_row - 1)

    pl.semaphore_wait(barrier, 1 + 2 * has_up.astype(jnp.int32) + 2 * has_down.astype(jnp.int32))

    @pl.when(has_up)
    def _():
        marks_to(1, 0, region, lat - 1).start()
        marks_to(1, 1, land, lat - 1).start()
        row_up(0).start()

    @pl.when(has_down)
    def _():
        marks_to(0, 0, region, lat + 1).start()
        marks_to(0, 1, land, lat + 1).start()
        row_down(0).start()

    for k in range(1, PRE):
        take_row(k)
        take_row(n_row - 1 - k)

        @pl.when(has_up)
        def _():
            row_up(k).start()

        @pl.when(has_down)
        def _():
            row_down(k).start()

    columns = [
        jnp.broadcast_to(table[lev, :, k : k + 1], (pad_lev, n_lon))
        for k in range(table.shape[2])
    ]

    def coefficient(region_row, land_row):
        region_row = jnp.broadcast_to(region_row, (pad_lev, n_lon))
        total = columns[0]
        for k in range(1, len(columns)):
            total = jnp.where(region_row == k, columns[k], total)
        return total * (1.0 - 0.6 * land_row.astype(F32))

    for r in range(n_row):
        ef[first + r] = coefficient(region[r : r + 1, :], land[r : r + 1, :])

    def faces_north(i):
        nf[i] = jnp.sqrt(ef[i] * ef[i + 1])

    def faces_east(i):
        c = ef[i]
        ef[i] = jnp.sqrt(c * pltpu.roll(c, n_lon - 1, 1))

    for i in range(first, last):
        faces_north(i)

    def step_rows(src, dst, i, store=None):
        def body(v, carry):
            for s in range(0, pad_lev, 16):
                rows = pl.ds(pl.multiple_of(v * pad_lev + s, 16), 16)
                f = src[i, rows, :]
                east = ef[i, s : s + 16, :] * (pltpu.roll(f, n_lon - 1, 1) - f)
                zonal = east - pltpu.roll(east, 1, 1)
                north = nf[i, s : s + 16, :] * (src[i + 1, rows, :] - f)
                south = nf[i - 1, s : s + 16, :] * (f - src[i - 1, rows, :])
                value = f + zonal + (north - south)
                if store is None:
                    dst[i, rows, :] = value
                else:
                    store(v, s, rows, value)
            return carry

        lax.fori_loop(0, n_var, body, 0)

    def loop_rows(low, high, fn):
        def body(i, carry):
            fn(i)
            return carry

        lax.fori_loop(low, high, body, 0)

    for side in range(2):
        exists = has_up if side == 0 else has_down

        @pl.when(exists)
        def _():
            for which in range(2):
                marks_to(side, which, region, lat).wait_recv()
            for k in range(PRE):
                r = n_row - 1 - k if side == 0 else k
                i = first - 1 - k if side == 0 else last + 1 + k
                ef[i] = coefficient(
                    marks[side, 0, r : r + 1, :], marks[side, 1, r : r + 1, :]
                )

        @pl.when(jnp.logical_not(exists))
        def _():
            for k in range(PRE):
                i = first - 1 - k if side == 0 else last + 1 + k
                ef[i] = jnp.zeros((pad_lev, n_lon), F32)
                f0[i] = jnp.zeros((feat, n_lon), F32)

    for i in list(range(0, first)) + list(range(last, last + PRE)):
        faces_north(i)
    for i in range(0, last + PRE + 1):
        faces_east(i)

    loop_rows(first + 1, last, lambda i: step_rows(f0, f1, i))
    loop_rows(first + 2, last - 1, lambda i: step_rows(f1, f2, i))
    loop_rows(first + 3, last - 2, lambda i: step_rows(f2, f3, i))

    loads[0].wait()
    loads[1].wait()
    n_feat = w_in.shape[1]
    for j in range(2):
        f_id = lax.broadcasted_iota(jnp.int32, (n_feat, feat), 0)
        c_id = lax.broadcasted_iota(jnp.int32, (n_feat, feat), 1)
        l_id = c_id % pad_lev
        want = (c_id // pad_lev) * (2 * n_lev) + j * n_lev + l_id
        pick = jnp.where((f_id == want) & (l_id < n_lev), 1.0, 0.0).astype(BF)
        wi[j] = jnp.dot(w_in[...], pick, preferred_element_type=F32).astype(BF)
        f_id = lax.broadcasted_iota(jnp.int32, (feat, n_feat), 1)
        c_id = lax.broadcasted_iota(jnp.int32, (feat, n_feat), 0)
        l_id = c_id % pad_lev
        want = (c_id // pad_lev) * (2 * n_lev) + j * n_lev + l_id
        pick = jnp.where((f_id == want) & (l_id < n_lev), 1.0, 0.0).astype(BF)
        wo[j] = jnp.dot(pick, w_out[...], preferred_element_type=F32).astype(BF)
    loads[2].wait()

    tile = 256

    def with_bias(x, start, size):
        b = bias[start : start + size, :]
        return x + jnp.concatenate([b] * (n_lon // b.shape[1]), axis=1)

    def profile_copy(p):
        return pltpu.make_async_remote_copy(
            src_ref=prof.at[peer, p], dst_ref=other.at[p],
            send_sem=prof_send.at[p], recv_sem=prof_recv.at[p],
            device_id={"lev": peer}, device_id_type=MESH,
        )

    def flux_row(owner, p):
        return half - 1 - p + owner * (1 + 2 * p)

    def flux_copy(p):
        return pltpu.make_async_remote_copy(
            src_ref=flux_own.at[p, peer], dst_ref=flux.at[flux_row(lev, p) + POST],
            send_sem=flux_send.at[p], recv_sem=flux_recv.at[p],
            device_id={"lev": peer}, device_id_type=MESH,
        )

    def edge_copy(p, j):
        q = p - (half - POST)
        place = flux_row(lev, p) + POST + (1 - 2 * lev) * n_row
        return pltpu.make_async_remote_copy(
            src_ref=flux_own.at[p, j], dst_ref=flux.at[place],
            send_sem=edge_send.at[q, j], recv_sem=edge_recv.at[peer, q],
            device_id={"lat": lat - 1 + 2 * lev, "lev": j}, device_id_type=MESH,
        )

    has_edge = jnp.where(lev == 0, has_up, has_down)

    def phase(p, carry):
        for side in range(2):
            exists = has_up if side == 0 else has_down

            @pl.when(exists)
            def _():
                if side == 0:
                    row_down(p).wait_recv()
                    f0[first - 1 - p] = halo[0, p].astype(F32)
                else:
                    row_up(p).wait_recv()
                    f0[last + 1 + p] = halo[1, p].astype(F32)

        def save(side):
            def store(v, s, rows, value):
                prof[side, p, rows, :] = value.astype(BF)

            return store

        for side in range(2):
            at = lambda k: first - p + k if side == 0 else last + p - k
            step_rows(f0, f1, at(0))
            step_rows(f1, f2, at(1))
            step_rows(f2, f3, at(2))
            step_rows(f3, None, at(3), save(side))
        exchange = profile_copy(p)
        exchange.start()
        exchange.wait_recv()

        for m in range(0, hid, tile):
            x = jnp.dot(wi[lev, m : m + tile, :], prof[lev, p], preferred_element_type=F32)
            x = x + jnp.dot(
                wi[peer, m : m + tile, :], other[p], preferred_element_type=F32
            )
            h1[m : m + tile, :] = gelu(with_bias(x, m, tile)).astype(BF)
        now, then = h1, h2
        for layer in range(n_mid):
            for m in range(0, hid, tile):
                x = jnp.dot(w_mid[layer, m : m + tile, :], now[...], preferred_element_type=F32)
                x = with_bias(x, (layer + 1) * hid + m, tile)
                then[m : m + tile, :] = gelu(x).astype(BF)
            now, then = then, now
        for j in range(2):
            x = jnp.dot(wo[j], now[...], preferred_element_type=F32)
            flux_own[p, j] = with_bias(x, (n_mid + 1) * hid + j * feat, feat).astype(BF)
        flux[flux_row(lev, p) + POST] = flux_own[p, lev]
        flux_copy(p).start()

        @pl.when(has_edge & (p >= half - POST))
        def _():
            for j in range(2):
                edge_copy(p, j).start()

        return carry

    lax.fori_loop(0, PRE, phase, 0)

    for p in range(half):
        flux_copy(p).wait_recv()

    def widen(i):
        f0[i] = flux[i - PRE + POST].astype(F32)

    loop_rows(first, last + 1, widen)

    def finish(i):
        def store(v, s, rows, value):
            count = min(16, n_lev - s)
            base = v * (n_lev * n_row) + s * n_row + (i - first)
            for c in range(n_split):
                split[c, pl.ds(base, count, stride=n_row), :] = value[
                    :count, c * lanes : (c + 1) * lanes
                ]

        step_rows(f1, None, i, store)

    loop_rows(first + 1, last, lambda i: step_rows(f0, f1, i))
    loop_rows(first + 2, last - 1, finish)

    for side in range(2):
        exists = has_up if side == 0 else has_down

        @pl.when(exists)
        def _():
            for q in range(POST):
                pltpu.make_async_remote_copy(
                    src_ref=flux_own.at[0, 0], dst_ref=flux.at[0],
                    send_sem=edge_send.at[0, 0], recv_sem=edge_recv.at[side, q],
                    device_id={"lev": peer}, device_id_type=MESH,
                ).wait_recv()
            for q in range(POST):
                widen(first - 1 - q if side == 0 else last + 1 + q)

    for i in (first - 1, first, last, last + 1):
        step_rows(f0, f1, i)
    for i in (first, first + 1, last - 1, last):
        finish(i)
    results = [
        pltpu.make_async_copy(split.at[c], columns_of(out, c), out_sem.at[c])
        for c in range(n_split)
    ]
    for piece in results:
        piece.start()

    for k in range(PRE):
        profile_copy(k).wait_send()
        flux_copy(k).wait_send()

    @pl.when(has_up)
    def _():
        for which in range(2):
            marks_to(1, which, region, lat).wait_send()
        for k in range(PRE):
            row_up(k).wait_send()

    @pl.when(has_down)
    def _():
        for which in range(2):
            marks_to(0, which, region, lat).wait_send()
        for k in range(PRE):
            row_down(k).wait_send()

    @pl.when(has_edge)
    def _():
        for p in range(half - POST, half):
            for j in range(2):
                edge_copy(p, j).wait_send()

    for piece in results:
        piece.wait()


def per_device(n_lat, fields, region, land, coef_table, w_in, b_in, w_mid, b_mid, w_out, b_out):
    n_var, n_lev, n_row, n_lon = fields.shape
    hid = w_in.shape[0]
    pad_lev = -(-n_lev // 16) * 16
    extra = pad_lev - n_lev
    feat = n_var * pad_lev
    rows = n_row + 2 * PRE
    table = jnp.pad(coef_table.reshape(2, n_lev, -1), ((0, 0), (0, extra), (0, 0)))
    last_bias = jnp.pad(b_out.reshape(n_var, 2, n_lev), ((0, 0), (0, 0), (0, extra)))
    bias = jnp.concatenate(
        [b_in, b_mid.reshape(-1), last_bias.transpose(1, 0, 2).reshape(-1)]
    )
    bias = jnp.broadcast_to(bias[:, None], (bias.shape[0], 128))
    dma = pltpu.SemaphoreType.DMA
    vmem = pl.BlockSpec(memory_space=pltpu.VMEM)
    hbm = pl.BlockSpec(memory_space=pl.ANY)
    result = pl.pallas_call(
        functools.partial(kernel, n_lat, n_var, n_lev, n_row),
        out_shape=jax.ShapeDtypeStruct((n_var * n_lev * n_row, n_lon), F32),
        in_specs=[vmem] * 4 + [hbm] * 4,
        out_specs=hbm,
        scratch_shapes=[
            pltpu.VMEM((n_lon // 128, n_var * n_lev * n_row, 128), F32),
            pltpu.VMEM(w_in.shape, BF),
            pltpu.VMEM(w_mid.shape, BF),
            pltpu.VMEM(w_out.shape, BF),
            pltpu.VMEM((2, hid, feat), BF),
            pltpu.VMEM((2, feat, hid), BF),
            pltpu.VMEM((n_row, feat, n_lon), BF),
            pltpu.VMEM((2, PRE, feat, n_lon), BF),
            pltpu.VMEM((2, 2, n_row, n_lon), jnp.int32),
            pltpu.VMEM((rows, feat, n_lon), F32),
            pltpu.VMEM((rows, feat, n_lon), F32),
            pltpu.VMEM((rows, feat, n_lon), F32),
            pltpu.VMEM((rows, feat, n_lon), F32),
            pltpu.VMEM((rows, pad_lev, n_lon), F32),
            pltpu.VMEM((rows, pad_lev, n_lon), F32),
            pltpu.VMEM((2, PRE, feat, n_lon), BF),
            pltpu.VMEM((PRE, feat, n_lon), BF),
            pltpu.VMEM((hid, n_lon), BF),
            pltpu.VMEM((hid, n_lon), BF),
            pltpu.VMEM((PRE, 2, feat, n_lon), BF),
            pltpu.VMEM((n_row + 2 * POST, feat, n_lon), BF),
            dma((n_lon // 128,)),
            dma((n_lon // 128,)),
            dma((3,)),
            dma((2, 2)),
            dma((2, 2)),
            dma((2, PRE)),
            dma((2, PRE)),
            dma((PRE,)),
            dma((PRE,)),
            dma((PRE,)),
            dma((PRE,)),
            dma((POST, 2)),
            dma((2, POST)),
        ],
        compiler_params=pltpu.CompilerParams(
            collective_id=0, has_side_effects=True, vmem_limit_bytes=60 * 2**20
        ),
    )(
        region, land, table, bias, fields.reshape(n_var * n_lev * n_row, n_lon),
        w_in, w_mid, w_out,
    )
    return result.reshape(fields.shape)


def solution(mesh):
    placed = (
        P(None, "lev", ("parts", "lat"), None),
        P(("parts", "lat"), None),
        P(("parts", "lat"), None),
    ) + (P(),) * 7
    return jax.shard_map(
        functools.partial(per_device, mesh.shape["lat"]),
        mesh=mesh,
        in_specs=placed,
        out_specs=P(None, "lev", ("parts", "lat"), None),
        check_vma=False,
    )
```

```python
import functools

import jax
import jax.numpy as jnp
from jax import lax
from jax.experimental import pallas as pl
from jax.experimental.pallas import tpu as pltpu
from jax.sharding import PartitionSpec as P

PRE = 4
POST = 2
MESH = pl.DeviceIdType.MESH
BF = jnp.bfloat16
F32 = jnp.float32


def gelu(x):
    scale = 0.7978845608028654
    inner = x * (scale + (scale * 0.044715) * (x * x))
    half = 0.5 * x
    return half + half * jnp.tanh(inner)


def kernel(
    n_lat, n_var, n_lev, n_row,
    region, land, table, b_in, b_mid, b_out, fields, w_in_hbm, w_mid_hbm, w_out_hbm,
    out,
    split, w_in, w_mid, w_out, wi, wo,
    sent, halo, marks, f0, f1, f2, f3, ef, ew, nf, prof, other, h1, h2, flux_own, flux, bias,
    in_sem, out_sem, w_sem, mark_send, mark_recv, halo_send, halo_recv, prof_send, prof_recv,
    flux_send, flux_recv, edge_send, edge_recv,
):
    lat = lax.axis_index("lat")
    lev = lax.axis_index("lev")
    peer = 1 - lev
    has_up = lat > 0
    has_down = lat < n_lat - 1
    pad_lev = ef.shape[1]
    feat = n_var * pad_lev
    n_lon = out.shape[1]
    hid = w_mid.shape[1]
    n_mid = w_mid.shape[0]
    half = n_row // 2
    first = PRE
    last = PRE + n_row - 1

    lanes = split.shape[2]
    n_split = split.shape[0]

    def columns_of(ref, c):
        return ref.at[:, c * lanes : (c + 1) * lanes]

    pieces = [
        pltpu.make_async_copy(columns_of(fields, c), split.at[c], in_sem.at[c])
        for c in range(n_split)
    ]
    for piece in pieces:
        piece.start()
    loads = [
        pltpu.make_async_copy(w_in_hbm, w_in, w_sem.at[0]),
        pltpu.make_async_copy(w_out_hbm, w_out, w_sem.at[1]),
        pltpu.make_async_copy(w_mid_hbm, w_mid, w_sem.at[2]),
    ]
    for load in loads:
        load.start()

    barrier = pltpu.get_barrier_semaphore()
    pl.semaphore_signal(barrier, inc=1, device_id={"lev": peer}, device_id_type=MESH)

    @pl.when(has_up)
    def _():
        for j in range(2):
            pl.semaphore_signal(
                barrier, inc=1, device_id={"lat": lat - 1, "lev": j}, device_id_type=MESH
            )

    @pl.when(has_down)
    def _():
        for j in range(2):
            pl.semaphore_signal(
                barrier, inc=1, device_id={"lat": lat + 1, "lev": j}, device_id_type=MESH
            )

    def take_row(r):
        for v in range(n_var):
            base = v * n_lev * n_row
            values = jnp.concatenate(
                [split[c, pl.ds(base + r, n_lev, stride=n_row), :] for c in range(n_split)],
                axis=1,
            )
            values = jnp.concatenate(
                [values, jnp.zeros((pad_lev - n_lev, n_lon), F32)], axis=0
            )
            f0[PRE + r, v * pad_lev : (v + 1) * pad_lev, :] = values
            sent[r, v * pad_lev : (v + 1) * pad_lev, :] = values.astype(BF)

    def row_up(k):
        return pltpu.make_async_remote_copy(
            src_ref=sent.at[k], dst_ref=halo.at[1, k],
            send_sem=halo_send.at[1, k], recv_sem=halo_recv.at[1, k],
            device_id={"lat": lat - 1}, device_id_type=MESH,
        )

    def row_down(k):
        return pltpu.make_async_remote_copy(
            src_ref=sent.at[n_row - 1 - k], dst_ref=halo.at[0, k],
            send_sem=halo_send.at[0, k], recv_sem=halo_recv.at[0, k],
            device_id={"lat": lat + 1}, device_id_type=MESH,
        )

    def marks_to(side, which, source, target):
        return pltpu.make_async_remote_copy(
            src_ref=source, dst_ref=marks.at[side, which],
            send_sem=mark_send.at[side, which], recv_sem=mark_recv.at[side, which],
            device_id={"lat": target}, device_id_type=MESH,
        )

    for piece in pieces:
        piece.wait()
    take_row(0)
    take_row(n_row - 1)

    pl.semaphore_wait(barrier, 1 + 2 * has_up.astype(jnp.int32) + 2 * has_down.astype(jnp.int32))

    @pl.when(has_up)
    def _():
        marks_to(1, 0, region, lat - 1).start()
        marks_to(1, 1, land, lat - 1).start()
        row_up(0).start()

    @pl.when(has_down)
    def _():
        marks_to(0, 0, region, lat + 1).start()
        marks_to(0, 1, land, lat + 1).start()
        row_down(0).start()

    for k in range(1, PRE):
        take_row(k)
        take_row(n_row - 1 - k)

        @pl.when(has_up)
        def _():
            row_up(k).start()

        @pl.when(has_down)
        def _():
            row_down(k).start()

    n_region, all_lev = table.shape
    wide = jnp.concatenate([table[...], jnp.zeros((n_region, 128 - all_lev), F32)], axis=1)
    wide = pltpu.roll(wide, (128 - lev * n_lev) % 128, 1)
    wide = jnp.concatenate([wide] * (128 // n_region), axis=0).T[:pad_lev]
    level_id = lax.broadcasted_iota(jnp.int32, (pad_lev, 128), 0)
    wide = jnp.where(level_id < n_lev, wide, 0.0)
    columns = [
        jnp.broadcast_to(wide[:, k : k + 1], (pad_lev, n_lon)) for k in range(n_region)
    ]

    def coefficient(region_row, land_row):
        region_row = jnp.broadcast_to(region_row, (pad_lev, n_lon))
        total = columns[0]
        for k in range(1, len(columns)):
            total = jnp.where(region_row == k, columns[k], total)
        return total * (1.0 - 0.6 * land_row.astype(F32))

    for r in range(n_row):
        ef[first + r] = coefficient(region[r : r + 1, :], land[r : r + 1, :])

    def faces_north(i):
        nf[i] = jnp.sqrt(ef[i] * ef[i + 1])

    def faces_east(i):
        c = ef[i]
        east = jnp.sqrt(c * pltpu.roll(c, n_lon - 1, 1))
        ef[i] = east
        ew[i] = pltpu.roll(east, 1, 1)

    for i in range(first, last):
        faces_north(i)

    def step_rows(src, dst, i, store=None):
        size = 8 if store is None else 16
        for s in range(0, pad_lev, size):
            east = ef[i, s : s + size, :]
            west = ew[i, s : s + size, :]
            north = nf[i, s : s + size, :]
            south = nf[i - 1, s : s + size, :]
            for v in range(n_var):
                rows = slice(v * pad_lev + s, v * pad_lev + s + size)
                f = src[i, rows, :]
                zonal = east * (pltpu.roll(f, n_lon - 1, 1) - f) - west * (
                    f - pltpu.roll(f, 1, 1)
                )
                meridional = north * (src[i + 1, rows, :] - f) - south * (
                    f - src[i - 1, rows, :]
                )
                value = f + zonal + meridional
                if store is None:
                    dst[i, rows, :] = value
                else:
                    store(v, s, rows, value)

    def loop_rows(low, high, fn):
        def body(i, carry):
            fn(i)
            return carry

        lax.fori_loop(low, high, body, 0)

    for side in range(2):
        exists = has_up if side == 0 else has_down

        @pl.when(exists)
        def _():
            for which in range(2):
                marks_to(side, which, region, lat).wait_recv()
            for k in range(PRE):
                r = n_row - 1 - k if side == 0 else k
                i = first - 1 - k if side == 0 else last + 1 + k
                ef[i] = coefficient(
                    marks[side, 0, r : r + 1, :], marks[side, 1, r : r + 1, :]
                )

        @pl.when(jnp.logical_not(exists))
        def _():
            for k in range(PRE):
                i = first - 1 - k if side == 0 else last + 1 + k
                ef[i] = jnp.zeros((pad_lev, n_lon), F32)
                f0[i] = jnp.zeros((feat, n_lon), F32)

    for i in list(range(0, first)) + list(range(last, last + PRE)):
        faces_north(i)
    for i in range(0, last + PRE + 1):
        faces_east(i)

    loop_rows(first + 1, last, lambda i: step_rows(f0, f1, i))
    loop_rows(first + 2, last - 1, lambda i: step_rows(f1, f2, i))
    loop_rows(first + 3, last - 2, lambda i: step_rows(f2, f3, i))

    loads[0].wait()
    loads[1].wait()
    n_feat = w_out.shape[0]
    for j in range(2):
        f_id = lax.broadcasted_iota(jnp.int32, (feat, n_feat), 1)
        c_id = lax.broadcasted_iota(jnp.int32, (feat, n_feat), 0)
        l_id = c_id % pad_lev
        want = (c_id // pad_lev) * (2 * n_lev) + j * n_lev + l_id
        pick = jnp.where((f_id == want) & (l_id < n_lev), 1.0, 0.0).astype(BF)
        wi[j] = jnp.dot(pick, w_in[...], preferred_element_type=F32).T.astype(BF)
        wo[j] = jnp.dot(pick, w_out[...], preferred_element_type=F32).astype(BF)

    def tall(row):
        return jnp.broadcast_to(row, (128, 128)).T

    start = (n_mid + 1) * hid
    for m in range(0, n_feat, 128):
        count = min(128, n_feat - m)
        row = b_out[:, m : m + count]
        if count < 128:
            row = jnp.concatenate([row, jnp.zeros((1, 128 - count), F32)], axis=1)
        bias[m : m + 128, :] = tall(row)
    bias[start : start + 2 * feat, :] = jnp.zeros((2 * feat, 128), F32)
    for v in range(n_var):
        for j in range(2):
            place = start + j * feat + v * pad_lev
            origin = v * 2 * n_lev + j * n_lev
            bias[place : place + n_lev, :] = bias[origin : origin + n_lev, :]
    for m in range(0, hid, 128):
        bias[m : m + 128, :] = tall(b_in[:, m : m + 128])
        for layer in range(n_mid):
            start = (layer + 1) * hid + m
            bias[start : start + 128, :] = tall(b_mid[layer : layer + 1, m : m + 128])
    loads[2].wait()

    tile = 256

    def with_bias(x, start, size):
        b = bias[start : start + size, :]
        return x + jnp.concatenate([b] * (n_lon // b.shape[1]), axis=1)

    def profile_copy(p):
        return pltpu.make_async_remote_copy(
            src_ref=prof.at[peer, p], dst_ref=other.at[p],
            send_sem=prof_send.at[p], recv_sem=prof_recv.at[p],
            device_id={"lev": peer}, device_id_type=MESH,
        )

    def flux_row(owner, p):
        return half - 1 - p + owner * (1 + 2 * p)

    def flux_copy(p):
        return pltpu.make_async_remote_copy(
            src_ref=flux_own.at[p, peer], dst_ref=flux.at[flux_row(lev, p) + POST],
            send_sem=flux_send.at[p], recv_sem=flux_recv.at[p],
            device_id={"lev": peer}, device_id_type=MESH,
        )

    def edge_copy(p, j):
        q = p - (half - POST)
        place = flux_row(lev, p) + POST + (1 - 2 * lev) * n_row
        return pltpu.make_async_remote_copy(
            src_ref=flux_own.at[p, j], dst_ref=flux.at[place],
            send_sem=edge_send.at[q, j], recv_sem=edge_recv.at[peer, q],
            device_id={"lat": lat - 1 + 2 * lev, "lev": j}, device_id_type=MESH,
        )

    has_edge = jnp.where(lev == 0, has_up, has_down)

    def phase(p, carry):
        for side in range(2):
            exists = has_up if side == 0 else has_down

            @pl.when(exists)
            def _():
                if side == 0:
                    row_down(p).wait_recv()
                    f0[first - 1 - p] = halo[0, p].astype(F32)
                else:
                    row_up(p).wait_recv()
                    f0[last + 1 + p] = halo[1, p].astype(F32)

        def save(side):
            def store(v, s, rows, value):
                prof[side, p, rows, :] = value.astype(BF)

            return store

        for k, (src, dst) in enumerate(((f0, f1), (f1, f2), (f2, f3), (f3, None))):
            for side in range(2):
                at = first - p + k if side == 0 else last + p - k
                step_rows(src, dst, at, save(side) if dst is None else None)
        exchange = profile_copy(p)
        exchange.start()
        exchange.wait_recv()

        for m in range(0, hid, tile):
            x = jnp.dot(wi[lev, m : m + tile, :], prof[lev, p], preferred_element_type=F32)
            x = x + jnp.dot(
                wi[peer, m : m + tile, :], other[p], preferred_element_type=F32
            )
            h1[m : m + tile, :] = gelu(with_bias(x, m, tile)).astype(BF)
        now, then = h1, h2
        for layer in range(n_mid):
            for m in range(0, hid, tile):
                x = jnp.dot(w_mid[layer, m : m + tile, :], now[...], preferred_element_type=F32)
                x = with_bias(x, (layer + 1) * hid + m, tile)
                then[m : m + tile, :] = gelu(x).astype(BF)
            now, then = then, now
        for j in range(2):
            x = jnp.dot(wo[j], now[...], preferred_element_type=F32)
            flux_own[p, j] = with_bias(x, (n_mid + 1) * hid + j * feat, feat).astype(BF)
        flux[flux_row(lev, p) + POST] = flux_own[p, lev]
        flux_copy(p).start()

        @pl.when(has_edge & (p >= half - POST))
        def _():
            for j in range(2):
                edge_copy(p, j).start()

        return carry

    lax.fori_loop(0, PRE, phase, 0)

    for p in range(half):
        flux_copy(p).wait_recv()

    def widen(i):
        f0[i] = flux[i - PRE + POST].astype(F32)

    loop_rows(first, last + 1, widen)

    def finish(i):
        def store(v, s, rows, value):
            count = min(16, n_lev - s)
            base = v * (n_lev * n_row) + s * n_row + (i - first)
            for c in range(n_split):
                split[c, pl.ds(base, count, stride=n_row), :] = value[
                    :count, c * lanes : (c + 1) * lanes
                ]

        step_rows(f1, None, i, store)

    loop_rows(first + 1, last, lambda i: step_rows(f0, f1, i))
    loop_rows(first + 2, last - 1, finish)

    for side in range(2):
        exists = has_up if side == 0 else has_down

        @pl.when(exists)
        def _():
            for q in range(POST):
                pltpu.make_async_remote_copy(
                    src_ref=flux_own.at[0, 0], dst_ref=flux.at[0],
                    send_sem=edge_send.at[0, 0], recv_sem=edge_recv.at[side, q],
                    device_id={"lev": peer}, device_id_type=MESH,
                ).wait_recv()
            for q in range(POST):
                widen(first - 1 - q if side == 0 else last + 1 + q)

    for i in (first - 1, first, last, last + 1):
        step_rows(f0, f1, i)
    for i in (first, first + 1, last - 1, last):
        finish(i)
    results = [
        pltpu.make_async_copy(split.at[c], columns_of(out, c), out_sem.at[c])
        for c in range(n_split)
    ]
    for piece in results:
        piece.start()

    for k in range(PRE):
        profile_copy(k).wait_send()
        flux_copy(k).wait_send()

    @pl.when(has_up)
    def _():
        for which in range(2):
            marks_to(1, which, region, lat).wait_send()
        for k in range(PRE):
            row_up(k).wait_send()

    @pl.when(has_down)
    def _():
        for which in range(2):
            marks_to(0, which, region, lat).wait_send()
        for k in range(PRE):
            row_down(k).wait_send()

    @pl.when(has_edge)
    def _():
        for p in range(half - POST, half):
            for j in range(2):
                edge_copy(p, j).wait_send()

    for piece in results:
        piece.wait()


def per_device(n_lat, fields, region, land, coef_table, w_in, b_in, w_mid, b_mid, w_out, b_out):
    n_var, n_lev, n_row, n_lon = fields.shape
    hid = w_in.shape[0]
    pad_lev = -(-n_lev // 16) * 16
    feat = n_var * pad_lev
    rows = n_row + 2 * PRE
    dma = pltpu.SemaphoreType.DMA
    vmem = pl.BlockSpec(memory_space=pltpu.VMEM)
    hbm = pl.BlockSpec(memory_space=pl.ANY)
    result = pl.pallas_call(
        functools.partial(kernel, n_lat, n_var, n_lev, n_row),
        out_shape=jax.ShapeDtypeStruct((n_var * n_lev * n_row, n_lon), F32),
        in_specs=[vmem] * 6 + [hbm] * 4,
        out_specs=hbm,
        scratch_shapes=[
            pltpu.VMEM((n_lon // 128, n_var * n_lev * n_row, 128), F32),
            pltpu.VMEM(w_in.shape[::-1], BF),
            pltpu.VMEM(w_mid.shape, BF),
            pltpu.VMEM(w_out.shape, BF),
            pltpu.VMEM((2, hid, feat), BF),
            pltpu.VMEM((2, feat, hid), BF),
            pltpu.VMEM((n_row, feat, n_lon), BF),
            pltpu.VMEM((2, PRE, feat, n_lon), BF),
            pltpu.VMEM((2, 2, n_row, n_lon), jnp.int32),
            pltpu.VMEM((rows, feat, n_lon), F32),
            pltpu.VMEM((rows, feat, n_lon), F32),
            pltpu.VMEM((rows, feat, n_lon), F32),
            pltpu.VMEM((rows, feat, n_lon), F32),
            pltpu.VMEM((rows, pad_lev, n_lon), F32),
            pltpu.VMEM((rows, pad_lev, n_lon), F32),
            pltpu.VMEM((rows, pad_lev, n_lon), F32),
            pltpu.VMEM((2, PRE, feat, n_lon), BF),
            pltpu.VMEM((PRE, feat, n_lon), BF),
            pltpu.VMEM((hid, n_lon), BF),
            pltpu.VMEM((hid, n_lon), BF),
            pltpu.VMEM((PRE, 2, feat, n_lon), BF),
            pltpu.VMEM((n_row + 2 * POST, feat, n_lon), BF),
            pltpu.VMEM(((w_mid.shape[0] + 1) * hid + 2 * feat, 128), F32),
            dma((n_lon // 128,)),
            dma((n_lon // 128,)),
            dma((3,)),
            dma((2, 2)),
            dma((2, 2)),
            dma((2, PRE)),
            dma((2, PRE)),
            dma((PRE,)),
            dma((PRE,)),
            dma((PRE,)),
            dma((PRE,)),
            dma((POST, 2)),
            dma((2, POST)),
        ],
        compiler_params=pltpu.CompilerParams(
            collective_id=0, has_side_effects=True, vmem_limit_bytes=60 * 2**20
        ),
    )(
        region, land, coef_table.T, b_in.reshape(1, -1), b_mid, b_out.reshape(1, -1),
        fields.reshape(n_var * n_lev * n_row, n_lon), w_in.T, w_mid, w_out,
    )
    return result.reshape(fields.shape)


def solution(mesh):
    placed = (
        P(None, "lev", ("parts", "lat"), None),
        P(("parts", "lat"), None),
        P(("parts", "lat"), None),
    ) + (P(),) * 7
    return jax.shard_map(
        functools.partial(per_device, mesh.shape["lat"]),
        mesh=mesh,
        in_specs=placed,
        out_specs=P(None, "lev", ("parts", "lat"), None),
        check_vma=False,
    )
```

```python
import functools

import jax
import jax.numpy as jnp
from jax import lax
from jax.experimental import pallas as pl
from jax.experimental.pallas import tpu as pltpu
from jax.sharding import PartitionSpec as P

PRE = 4
POST = 2
MESH = pl.DeviceIdType.MESH
BF = jnp.bfloat16
F32 = jnp.float32


def gelu(x):
    scale = 0.7978845608028654
    inner = x * (scale + (scale * 0.044715) * (x * x))
    half = 0.5 * x
    return half + half * jnp.tanh(inner)


def kernel(
    n_lat, n_var, n_lev, n_row,
    region, land, table, b_in, b_mid, b_out, fields, w_in_hbm, w_mid_hbm, w_out_hbm,
    out,
    split, w_in, w_mid, w_out, wi, wo,
    sent, halo, marks, f0, f1, f2, f3, ef, ew, nf, prof, other, h1, h2, flux_own, flux, bias,
    in_sem, out_sem, w_sem, mark_send, mark_recv, halo_send, halo_recv, prof_send, prof_recv,
    flux_send, flux_recv, edge_send, edge_recv,
):
    lat = lax.axis_index("lat")
    lev = lax.axis_index("lev")
    peer = 1 - lev
    has_up = lat > 0
    has_down = lat < n_lat - 1
    pad_lev = ef.shape[1]
    feat = n_var * pad_lev
    n_lon = out.shape[1]
    hid = w_mid.shape[1]
    n_mid = w_mid.shape[0]
    half = n_row // 2
    first = PRE
    last = PRE + n_row - 1

    lanes = split.shape[2]
    n_split = split.shape[0]

    def columns_of(ref, c):
        return ref.at[:, c * lanes : (c + 1) * lanes]

    pieces = [
        pltpu.make_async_copy(columns_of(fields, c), split.at[c], in_sem.at[c])
        for c in range(n_split)
    ]
    for piece in pieces:
        piece.start()
    loads = [
        pltpu.make_async_copy(w_in_hbm, w_in, w_sem.at[0]),
        pltpu.make_async_copy(w_out_hbm, w_out, w_sem.at[1]),
        pltpu.make_async_copy(w_mid_hbm, w_mid, w_sem.at[2]),
    ]
    for load in loads:
        load.start()

    barrier = pltpu.get_barrier_semaphore()
    pl.semaphore_signal(barrier, inc=1, device_id={"lev": peer}, device_id_type=MESH)

    @pl.when(has_up)
    def _():
        for j in range(2):
            pl.semaphore_signal(
                barrier, inc=1, device_id={"lat": lat - 1, "lev": j}, device_id_type=MESH
            )

    @pl.when(has_down)
    def _():
        for j in range(2):
            pl.semaphore_signal(
                barrier, inc=1, device_id={"lat": lat + 1, "lev": j}, device_id_type=MESH
            )

    def take_row(r):
        for v in range(n_var):
            base = v * n_lev * n_row
            values = jnp.concatenate(
                [split[c, pl.ds(base + r, n_lev, stride=n_row), :] for c in range(n_split)],
                axis=1,
            )
            values = jnp.concatenate(
                [values, jnp.zeros((pad_lev - n_lev, n_lon), F32)], axis=0
            )
            f0[PRE + r, v * pad_lev : (v + 1) * pad_lev, :] = values
            sent[r, v * pad_lev : (v + 1) * pad_lev, :] = values.astype(BF)

    cut = feat // 2

    def row_up(k, h):
        part = pl.ds(h * cut, cut)
        return pltpu.make_async_remote_copy(
            src_ref=sent.at[k, part], dst_ref=halo.at[1, k, part],
            send_sem=halo_send.at[1, k, h], recv_sem=halo_recv.at[1, k, h],
            device_id={"lat": lat - 1}, device_id_type=MESH,
        )

    def row_down(k, h):
        part = pl.ds(h * cut, cut)
        return pltpu.make_async_remote_copy(
            src_ref=sent.at[n_row - 1 - k, part], dst_ref=halo.at[0, k, part],
            send_sem=halo_send.at[0, k, h], recv_sem=halo_recv.at[0, k, h],
            device_id={"lat": lat + 1}, device_id_type=MESH,
        )

    def marks_to(side, which, source, target):
        return pltpu.make_async_remote_copy(
            src_ref=source, dst_ref=marks.at[side, which],
            send_sem=mark_send.at[side, which], recv_sem=mark_recv.at[side, which],
            device_id={"lat": target}, device_id_type=MESH,
        )

    for piece in pieces:
        piece.wait()
    take_row(0)
    take_row(n_row - 1)

    pl.semaphore_wait(barrier, 1 + 2 * has_up.astype(jnp.int32) + 2 * has_down.astype(jnp.int32))

    @pl.when(has_up)
    def _():
        marks_to(1, 0, region, lat - 1).start()
        marks_to(1, 1, land, lat - 1).start()
        row_up(0, 0).start()
        row_up(0, 1).start()

    @pl.when(has_down)
    def _():
        marks_to(0, 0, region, lat + 1).start()
        marks_to(0, 1, land, lat + 1).start()
        row_down(0, 0).start()
        row_down(0, 1).start()

    for k in range(1, PRE):
        take_row(k)
        take_row(n_row - 1 - k)
        if k == 1:

            @pl.when(has_up)
            def _():
                row_up(1, 0).start()

            @pl.when(has_down)
            def _():
                row_down(1, 0).start()

    n_region, all_lev = table.shape
    wide = jnp.concatenate([table[...], jnp.zeros((n_region, 128 - all_lev), F32)], axis=1)
    wide = pltpu.roll(wide, (128 - lev * n_lev) % 128, 1)
    wide = jnp.concatenate([wide] * (128 // n_region), axis=0).T[:pad_lev]
    level_id = lax.broadcasted_iota(jnp.int32, (pad_lev, 128), 0)
    wide = jnp.where(level_id < n_lev, wide, 0.0)
    columns = [
        jnp.broadcast_to(wide[:, k : k + 1], (pad_lev, n_lon)) for k in range(n_region)
    ]

    def coefficient(region_row, land_row):
        region_row = jnp.broadcast_to(region_row, (pad_lev, n_lon))
        total = columns[0]
        for k in range(1, len(columns)):
            total = jnp.where(region_row == k, columns[k], total)
        return total * (1.0 - 0.6 * land_row.astype(F32))

    for r in range(n_row):
        ef[first + r] = coefficient(region[r : r + 1, :], land[r : r + 1, :])

    def faces_north(i):
        nf[i] = jnp.sqrt(ef[i] * ef[i + 1])

    def faces_east(i):
        c = ef[i]
        east = jnp.sqrt(c * pltpu.roll(c, n_lon - 1, 1))
        ef[i] = east
        ew[i] = pltpu.roll(east, 1, 1)

    for i in range(first, last):
        faces_north(i)

    def step_rows(src, dst, i, store=None):
        size = 8 if store is None else 16
        for s in range(0, pad_lev, size):
            east = ef[i, s : s + size, :]
            west = ew[i, s : s + size, :]
            north = nf[i, s : s + size, :]
            south = nf[i - 1, s : s + size, :]
            for v in range(n_var):
                rows = slice(v * pad_lev + s, v * pad_lev + s + size)
                f = src[i, rows, :]
                zonal = east * (pltpu.roll(f, n_lon - 1, 1) - f) - west * (
                    f - pltpu.roll(f, 1, 1)
                )
                meridional = north * (src[i + 1, rows, :] - f) - south * (
                    f - src[i - 1, rows, :]
                )
                value = f + zonal + meridional
                if store is None:
                    dst[i, rows, :] = value
                else:
                    store(v, s, rows, value)

    def loop_rows(low, high, fn):
        def body(i, carry):
            fn(i)
            return carry

        lax.fori_loop(low, high, body, 0)

    for side in range(2):
        exists = has_up if side == 0 else has_down

        @pl.when(exists)
        def _():
            for which in range(2):
                marks_to(side, which, region, lat).wait_recv()
            for k in range(PRE):
                r = n_row - 1 - k if side == 0 else k
                i = first - 1 - k if side == 0 else last + 1 + k
                ef[i] = coefficient(
                    marks[side, 0, r : r + 1, :], marks[side, 1, r : r + 1, :]
                )

        @pl.when(jnp.logical_not(exists))
        def _():
            for k in range(PRE):
                i = first - 1 - k if side == 0 else last + 1 + k
                ef[i] = jnp.zeros((pad_lev, n_lon), F32)
                f0[i] = jnp.zeros((feat, n_lon), F32)

    for i in list(range(0, first)) + list(range(last, last + PRE)):
        faces_north(i)
    for i in range(0, last + PRE + 1):
        faces_east(i)

    loop_rows(first + 1, last, lambda i: step_rows(f0, f1, i))
    loop_rows(first + 2, last - 1, lambda i: step_rows(f1, f2, i))
    loop_rows(first + 3, last - 2, lambda i: step_rows(f2, f3, i))

    loads[0].wait()
    loads[1].wait()
    n_feat = w_out.shape[0]
    for j in range(2):
        f_id = lax.broadcasted_iota(jnp.int32, (feat, n_feat), 1)
        c_id = lax.broadcasted_iota(jnp.int32, (feat, n_feat), 0)
        l_id = c_id % pad_lev
        want = (c_id // pad_lev) * (2 * n_lev) + j * n_lev + l_id
        pick = jnp.where((f_id == want) & (l_id < n_lev), 1.0, 0.0).astype(BF)
        wi[j] = jnp.dot(pick, w_in[...], preferred_element_type=F32).T.astype(BF)
        wo[j] = jnp.dot(pick, w_out[...], preferred_element_type=F32).astype(BF)

    def tall(row):
        return jnp.broadcast_to(row, (128, 128)).T

    start = (n_mid + 1) * hid
    for m in range(0, n_feat, 128):
        count = min(128, n_feat - m)
        row = b_out[:, m : m + count]
        if count < 128:
            row = jnp.concatenate([row, jnp.zeros((1, 128 - count), F32)], axis=1)
        bias[m : m + 128, :] = tall(row)
    bias[start : start + 2 * feat, :] = jnp.zeros((2 * feat, 128), F32)
    for v in range(n_var):
        for j in range(2):
            place = start + j * feat + v * pad_lev
            origin = v * 2 * n_lev + j * n_lev
            bias[place : place + n_lev, :] = bias[origin : origin + n_lev, :]
    for m in range(0, hid, 128):
        bias[m : m + 128, :] = tall(b_in[:, m : m + 128])
        for layer in range(n_mid):
            start = (layer + 1) * hid + m
            bias[start : start + 128, :] = tall(b_mid[layer : layer + 1, m : m + 128])
    loads[2].wait()

    tile = 256

    def with_bias(x, start, size):
        b = bias[start : start + size, :]
        return x + jnp.concatenate([b] * (n_lon // b.shape[1]), axis=1)

    def profile_copy(p):
        return pltpu.make_async_remote_copy(
            src_ref=prof.at[peer, p], dst_ref=other.at[p],
            send_sem=prof_send.at[p], recv_sem=prof_recv.at[p],
            device_id={"lev": peer}, device_id_type=MESH,
        )

    def flux_row(owner, p):
        return half - 1 - p + owner * (1 + 2 * p)

    def flux_copy(p):
        return pltpu.make_async_remote_copy(
            src_ref=flux_own.at[p, peer], dst_ref=flux.at[flux_row(lev, p) + POST],
            send_sem=flux_send.at[p], recv_sem=flux_recv.at[p],
            device_id={"lev": peer}, device_id_type=MESH,
        )

    def edge_copy(p, j):
        q = p - (half - POST)
        place = flux_row(lev, p) + POST + (1 - 2 * lev) * n_row
        return pltpu.make_async_remote_copy(
            src_ref=flux_own.at[p, j], dst_ref=flux.at[place],
            send_sem=edge_send.at[q, j], recv_sem=edge_recv.at[peer, q],
            device_id={"lat": lat - 1 + 2 * lev, "lev": j}, device_id_type=MESH,
        )

    has_edge = jnp.where(lev == 0, has_up, has_down)

    def phase(p, carry):
        for side in range(2):
            exists = has_up if side == 0 else has_down

            @pl.when(exists)
            def _():
                if side == 0:
                    row_down(p, 0).wait_recv()
                    row_down(p, 1).wait_recv()
                    f0[first - 1 - p] = halo[0, p].astype(F32)
                else:
                    row_up(p, 0).wait_recv()
                    row_up(p, 1).wait_recv()
                    f0[last + 1 + p] = halo[1, p].astype(F32)

        def save(side):
            def store(v, s, rows, value):
                prof[side, p, rows, :] = value.astype(BF)

            return store

        for k, (src, dst) in enumerate(((f0, f1), (f1, f2), (f2, f3), (f3, None))):
            for side in range(2):
                at = first - p + k if side == 0 else last + p - k
                step_rows(src, dst, at, save(side) if dst is None else None)
        exchange = profile_copy(p)
        exchange.start()

        for exists, row in ((has_up, row_up), (has_down, row_down)):

            @pl.when(exists & (p < PRE - 1))
            def _():
                row(p + 1, 1).start()

            @pl.when(exists & (p < PRE - 2))
            def _():
                row(p + 2, 0).start()

        @pl.when(has_edge & (p > half - POST))
        def _():
            edge_copy(p - 1, 1).start()

        exchange.wait_recv()

        for m in range(0, hid, tile):
            x = jnp.dot(wi[lev, m : m + tile, :], prof[lev, p], preferred_element_type=F32)
            x = x + jnp.dot(
                wi[peer, m : m + tile, :], other[p], preferred_element_type=F32
            )
            h1[m : m + tile, :] = gelu(with_bias(x, m, tile)).astype(BF)
        now, then = h1, h2
        for layer in range(n_mid):
            for m in range(0, hid, tile):
                x = jnp.dot(w_mid[layer, m : m + tile, :], now[...], preferred_element_type=F32)
                x = with_bias(x, (layer + 1) * hid + m, tile)
                then[m : m + tile, :] = gelu(x).astype(BF)
            now, then = then, now
        for j in range(2):
            x = jnp.dot(wo[j], now[...], preferred_element_type=F32)
            flux_own[p, j] = with_bias(x, (n_mid + 1) * hid + j * feat, feat).astype(BF)
        flux[flux_row(lev, p) + POST] = flux_own[p, lev]
        flux_copy(p).start()

        @pl.when(has_edge & (p >= half - POST))
        def _():
            edge_copy(p, 0).start()

        return carry

    lax.fori_loop(0, PRE, phase, 0)

    @pl.when(has_edge)
    def _():
        edge_copy(half - 1, 1).start()

    for p in range(half):
        flux_copy(p).wait_recv()

    def widen(i):
        f0[i] = flux[i - PRE + POST].astype(F32)

    loop_rows(first, last + 1, widen)

    def finish(i):
        def store(v, s, rows, value):
            count = min(16, n_lev - s)
            base = v * (n_lev * n_row) + s * n_row + (i - first)
            for c in range(n_split):
                split[c, pl.ds(base, count, stride=n_row), :] = value[
                    :count, c * lanes : (c + 1) * lanes
                ]

        step_rows(f1, None, i, store)

    loop_rows(first + 1, last, lambda i: step_rows(f0, f1, i))
    loop_rows(first + 2, last - 1, finish)

    for side in range(2):
        exists = has_up if side == 0 else has_down

        @pl.when(exists)
        def _():
            for q in range(POST):
                pltpu.make_async_remote_copy(
                    src_ref=flux_own.at[0, 0], dst_ref=flux.at[0],
                    send_sem=edge_send.at[0, 0], recv_sem=edge_recv.at[side, q],
                    device_id={"lev": peer}, device_id_type=MESH,
                ).wait_recv()
            for q in range(POST):
                widen(first - 1 - q if side == 0 else last + 1 + q)

    for i in (first - 1, first, last, last + 1):
        step_rows(f0, f1, i)
    for i in (first, first + 1, last - 1, last):
        finish(i)
    results = [
        pltpu.make_async_copy(split.at[c], columns_of(out, c), out_sem.at[c])
        for c in range(n_split)
    ]
    for piece in results:
        piece.start()

    for k in range(PRE):
        profile_copy(k).wait_send()
        flux_copy(k).wait_send()

    @pl.when(has_up)
    def _():
        for which in range(2):
            marks_to(1, which, region, lat).wait_send()
        for k in range(PRE):
            row_up(k, 0).wait_send()
            row_up(k, 1).wait_send()

    @pl.when(has_down)
    def _():
        for which in range(2):
            marks_to(0, which, region, lat).wait_send()
        for k in range(PRE):
            row_down(k, 0).wait_send()
            row_down(k, 1).wait_send()

    @pl.when(has_edge)
    def _():
        for p in range(half - POST, half):
            for j in range(2):
                edge_copy(p, j).wait_send()

    for piece in results:
        piece.wait()


def per_device(n_lat, fields, region, land, coef_table, w_in, b_in, w_mid, b_mid, w_out, b_out):
    n_var, n_lev, n_row, n_lon = fields.shape
    hid = w_in.shape[0]
    pad_lev = -(-n_lev // 16) * 16
    feat = n_var * pad_lev
    rows = n_row + 2 * PRE
    dma = pltpu.SemaphoreType.DMA
    vmem = pl.BlockSpec(memory_space=pltpu.VMEM)
    hbm = pl.BlockSpec(memory_space=pl.ANY)
    result = pl.pallas_call(
        functools.partial(kernel, n_lat, n_var, n_lev, n_row),
        out_shape=jax.ShapeDtypeStruct((n_var * n_lev * n_row, n_lon), F32),
        in_specs=[vmem] * 6 + [hbm] * 4,
        out_specs=hbm,
        scratch_shapes=[
            pltpu.VMEM((n_lon // 128, n_var * n_lev * n_row, 128), F32),
            pltpu.VMEM(w_in.shape[::-1], BF),
            pltpu.VMEM(w_mid.shape, BF),
            pltpu.VMEM(w_out.shape, BF),
            pltpu.VMEM((2, hid, feat), BF),
            pltpu.VMEM((2, feat, hid), BF),
            pltpu.VMEM((n_row, feat, n_lon), BF),
            pltpu.VMEM((2, PRE, feat, n_lon), BF),
            pltpu.VMEM((2, 2, n_row, n_lon), jnp.int32),
            pltpu.VMEM((rows, feat, n_lon), F32),
            pltpu.VMEM((rows, feat, n_lon), F32),
            pltpu.VMEM((rows, feat, n_lon), F32),
            pltpu.VMEM((rows, feat, n_lon), F32),
            pltpu.VMEM((rows, pad_lev, n_lon), F32),
            pltpu.VMEM((rows, pad_lev, n_lon), F32),
            pltpu.VMEM((rows, pad_lev, n_lon), F32),
            pltpu.VMEM((2, PRE, feat, n_lon), BF),
            pltpu.VMEM((PRE, feat, n_lon), BF),
            pltpu.VMEM((hid, n_lon), BF),
            pltpu.VMEM((hid, n_lon), BF),
            pltpu.VMEM((PRE, 2, feat, n_lon), BF),
            pltpu.VMEM((n_row + 2 * POST, feat, n_lon), BF),
            pltpu.VMEM(((w_mid.shape[0] + 1) * hid + 2 * feat, 128), F32),
            dma((n_lon // 128,)),
            dma((n_lon // 128,)),
            dma((3,)),
            dma((2, 2)),
            dma((2, 2)),
            dma((2, PRE, 2)),
            dma((2, PRE, 2)),
            dma((PRE,)),
            dma((PRE,)),
            dma((PRE,)),
            dma((PRE,)),
            dma((POST, 2)),
            dma((2, POST)),
        ],
        compiler_params=pltpu.CompilerParams(
            collective_id=0, has_side_effects=True, vmem_limit_bytes=60 * 2**20
        ),
    )(
        region, land, coef_table.T, b_in.reshape(1, -1), b_mid, b_out.reshape(1, -1),
        fields.reshape(n_var * n_lev * n_row, n_lon), w_in.T, w_mid, w_out,
    )
    return result.reshape(fields.shape)


def solution(mesh):
    placed = (
        P(None, "lev", ("parts", "lat"), None),
        P(("parts", "lat"), None),
        P(("parts", "lat"), None),
    ) + (P(),) * 7
    return jax.shard_map(
        functools.partial(per_device, mesh.shape["lat"]),
        mesh=mesh,
        in_specs=placed,
        out_specs=P(None, "lev", ("parts", "lat"), None),
        check_vma=False,
    )
```
